32 devices in a mesh: tx: 2 (over core), ty: 4 (over y, x), lz: 4 (over z).
Axes of the slice: x: 2, y: 2, z: 4, core: 2. Of those that a mesh axis runs over, the one named last changes fastest.
Arguments:
- test_field: bfloat16 [64, 6, 48, 512], P('tx', None, 'lz', 'ty'), may hold values from -6 to 6
- dir_field: bfloat16 [64, 6, 48, 512], P('tx', None, 'lz', 'ty'), may hold values from -6 to 6
- border_b: bfloat16 [64, 6, 48, 512], P('tx', None, 'lz', 'ty')
- border_c: bfloat16 [64, 6, 48, 512], P('tx', None, 'lz', 'ty')
- land_mask: int32 [64, 512], P('tx', 'ty'), may hold values from 0 to 1, as said below
- active_rows: int32 [64, 4], P('tx', 'ty'), may hold values from -1 to 31, as said below
- cell_blocks: bfloat16 [64, 36, 512], P('tx', None, 'ty'), may hold values from -2.5 to 2.5
- column_k: bfloat16 [288, 288], replicated, may hold values from -0.375 to 0.375
- kappa: float32 [6], replicated, may hold values from 0.2 to 1
Outputs:
- test_image: bfloat16 [64, 6, 48, 512], P('tx', None, 'lz', 'ty')
- dir_image: bfloat16 [64, 6, 48, 512], P('tx', None, 'lz', 'ty')
- border: float32 [3], replicated
The draws below stay inside these ranges and needn't reach their ends.
Inputs may be any that keep to these rules, and one draw needn't show every extreme that they name: `active_rows`: in each tile the 32 entries name distinct local rows, the active ones, followed by -1 for the rest; some tile has all 32 rows active. `land_mask`: cells whose latitude index y has y % 128 equal to 0 or 127 are ocean.
All inputs are finite; a program needn't handle non-finite values.
Results may differ from the reference program's by a relative error of at most 0.0028.
Values may be sent and summed in bfloat16 or wider, within the bound.
A program may use at most 192 MiB of HBM per device.

```python
import math
import jax
import jax.numpy as jnp
from jax import lax

NU = 6
NZ = 48
BLK = 128
TXD = 32
COL = 288
NX = 64
NY = 512


def border_law(key):
    shape = (NX, NU, NZ, NY)
    longitude = jnp.arange(NX, dtype=jnp.float32) / NX
    rising = jnp.exp(jnp.log(10.0) * longitude)[:, None, None, None]
    return jax.random.normal(key, shape, jnp.float32) * rising


def draw_border_b(key, part):
    return border_law(jax.random.fold_in(key, 11)).astype(jnp.bfloat16)


def draw_border_c(key, part):
    return border_law(jax.random.fold_in(key, 23)).astype(jnp.bfloat16)


def draw_land_mask(key, part):
    wet = jax.random.randint(jax.random.fold_in(key, 53), (NX, NY), 0, 10) < 7
    inside = jnp.arange(NY, dtype=jnp.int32) % BLK
    edges = (inside == 0) | (inside == BLK - 1)
    return jnp.where(edges[None, :], True, wet).astype(jnp.int32)


def draw_active_rows(key, part):
    tiles_x = NX // TXD
    tiles_y = NY // BLK
    first, second, third = jax.random.split(jax.random.fold_in(key, 37), 3)
    counts = jax.random.randint(first, (tiles_x * tiles_y,), 1, TXD + 1)
    full = jax.random.randint(second, (), 0, tiles_x * tiles_y)
    counts = counts.at[full].set(TXD)
    orders = jax.vmap(lambda k: jax.random.permutation(k, TXD))(jax.random.split(third, tiles_x * tiles_y))
    lines = jnp.arange(TXD, dtype=jnp.int32)
    entries = jnp.where(lines[None, :] < counts[:, None], orders.astype(jnp.int32), -1)
    entries = entries.reshape(tiles_x, tiles_y, TXD).transpose(0, 2, 1)
    return entries.reshape(NX, tiles_y).astype(jnp.int32)


def level_of(rng, dims, shards, smallest, largest):
    gain, own = 1.0, jax.random.fold_in(rng, 6)
    for position, parts in shards:
        draws = jnp.exp(jax.random.uniform(jax.random.fold_in(own, position), (parts,), jnp.float32, smallest / len(shards), largest / len(shards)))
        gain = gain * jnp.repeat(draws, dims[position] // parts).reshape([-1 if axis == position else 1 for axis in range(len(dims))])
    return gain


def noise(key, dims, scale, reach, shards=(), kind=jnp.bfloat16):
    gain = level_of(key, dims, shards, -0.22, 0.18) if shards else 1.0
    result = jax.random.normal(key, dims, jnp.float32) * scale * gain
    return jnp.minimum(jnp.maximum(result, -reach), reach).astype(kind)


def setup_inputs(seed: int = 0) -> dict:
    key_of = jax.random.split(jax.random.key(seed), 10)
    return {
        "test_field": noise(key_of[0], (NX, NU, NZ, NY), 1.0, 6.0, ((0, 2), (2, 4), (3, 4))),
        "dir_field": noise(key_of[1], (NX, NU, NZ, NY), 1.0, 6.0, ((0, 2), (2, 4), (3, 4))),
        "border_b": draw_border_b(jax.random.fold_in(key_of[9], 71), 0),
        "border_c": draw_border_c(jax.random.fold_in(key_of[9], 71), 0),
        "land_mask": draw_land_mask(jax.random.fold_in(key_of[9], 71), 0),
        "active_rows": draw_active_rows(jax.random.fold_in(key_of[9], 71), 0),
        "cell_blocks": noise(key_of[6], (NX, NU * NU, NY), NU ** -0.5, 2.5, ((0, 2), (2, 4))),
        "column_k": noise(key_of[7], (COL, COL), COL ** -0.5, 0.375),
        "kappa": jnp.clip(jnp.exp(jax.random.uniform(key_of[8], (NU,), jnp.float32, math.log(0.2), math.log(1.0))), 0.2, 1.0),
    }


def ocean_weight(land_mask, active_rows):
    tiles_x = NX // TXD
    tiles_y = active_rows.shape[1]
    lists = active_rows.reshape(tiles_x, TXD, tiles_y)
    lines = jnp.arange(TXD, dtype=jnp.int32)
    named = jnp.any(lists[:, :, None, :] == lines[None, None, :, None], axis=1)
    active = jnp.repeat(named.reshape(NX, tiles_y).astype(jnp.float32), BLK, axis=1)
    return land_mask.astype(jnp.float32) * active

def apply_jacobian(field, weight, cell_blocks, column_k, kappa):
    masked = field * weight.astype(jnp.bfloat16)[:, None, None, :]
    after = jnp.roll(masked, -1, axis=0)
    before = jnp.roll(masked, 1, axis=0)
    groups = NX // TXD
    dense = column_k.astype(jnp.float32)

    def one_group(items):
        center, ahead, behind, ocean, blocks = items
        here = center.astype(jnp.float32)
        coupled = jnp.einsum('pq,gqy->gpy', dense, here.reshape(TXD, COL, NY))
        coupled = lax.optimization_barrier(coupled.astype(jnp.bfloat16)).astype(jnp.float32)
        coupled = coupled.reshape(TXD, NU, NZ, NY)
        local = jnp.einsum('guwy,gwzy->guzy', blocks.astype(jnp.float32).reshape(TXD, NU, NU, NY), here)
        edge = jnp.zeros_like(here[..., :1])
        north = jnp.concatenate([here[..., 1:], edge], axis=3)
        south = jnp.concatenate([edge, here[..., :-1]], axis=3)
        spread = ahead.astype(jnp.float32) + behind.astype(jnp.float32) + north + south - 4.0 * here
        return ocean[:, None, None, :] * (coupled + local + kappa[None, :, None, None] * spread)
    shaped = (masked.reshape(groups, TXD, NU, NZ, NY), after.reshape(groups, TXD, NU, NZ, NY), before.reshape(groups, TXD, NU, NZ, NY), weight.reshape(groups, TXD, NY), cell_blocks.reshape(groups, TXD, NU * NU, NY))
    return lax.map(one_group, shaped).reshape(NX, NU, NZ, NY)

def reference(test_field, dir_field, border_b, border_c, land_mask, active_rows, cell_blocks, column_k, kappa):
    weight = ocean_weight(land_mask, active_rows)
    test_full = apply_jacobian(test_field, weight, cell_blocks, column_k, kappa)
    dir_full = apply_jacobian(dir_field, weight, cell_blocks, column_k, kappa)
    column_b = border_b.astype(jnp.float32)
    row_c = border_c.astype(jnp.float32)
    norm_b = jnp.sum(column_b * column_b)
    norm_c = jnp.sum(row_c * row_c)
    value_c = jnp.sum(row_c * test_field.astype(jnp.float32))
    value_a = jnp.sum(column_b * test_full)
    value_e = jnp.sum(column_b * dir_full)
    border = jnp.stack([value_a / jnp.sqrt(norm_b), value_e / jnp.sqrt(norm_b), value_c / jnp.sqrt(norm_c)])
    return (test_full.astype(jnp.bfloat16), dir_full.astype(jnp.bfloat16), border)
```

```python
import functools
import jax
import jax.numpy as jnp
from jax import lax
from jax.experimental import pallas as pl
from jax.experimental.pallas import tpu as pltpu
from jax.sharding import PartitionSpec as P

MESH = pl.DeviceIdType.MESH
F32 = jnp.float32
BF16 = jnp.bfloat16


def kernel(
    sizes, chunks,
    test_ref, dir_ref, b_ref, c_ref, land_ref, active_ref, blocks_ref, k_ref, kappa_ref,
    out_t, out_d, border_ref,
    masked, arrived, product, coupled, weight, rates, big_k, pack, spread_s, blocks_s,
    edge_out, edge_in, edge_f, stat_out, stat_z, stat_y, stat_x,
    fs, fr, bs, br, xs, xr, ys, yr, ss, sr_z, sr_y, sr_x,
):
    nx, ny, nz = sizes
    rows, units, layers, cells = test_ref.shape
    slab = units * layers
    full = 2 * slab
    group = rows // nz
    step = group // chunks
    mx, my, mz = lax.axis_index("tx"), lax.axis_index("ty"), lax.axis_index("lz")
    fields = (test_ref, dir_ref)

    barrier = pltpu.get_barrier_semaphore()
    for name, me, size in (("tx", mx, nx), ("ty", my, ny), ("lz", mz, nz)):
        for k in range(1, size):
            pl.semaphore_signal(
                barrier, inc=1, device_id={name: lax.rem(me + k, size)}, device_id_type=MESH
            )

    lane = lax.broadcasted_iota(jnp.int32, (full, cells), 1)
    active = jnp.broadcast_to(active_ref[...], (rows, cells))

    def pack_row(x, edges):
        named = jnp.max((active == x).astype(F32), axis=0, keepdims=True)
        row = land_ref[pl.ds(x, 1), :].astype(F32) * named
        weight[pl.ds(x, 1), :] = row
        for f in range(2):
            for u in range(units):
                value = fields[f][x, u].astype(F32) * row
                pack[pl.ds(f * slab + u * layers, layers), :] = value
        value = pack[...]
        masked[x + 1] = value.astype(BF16)
        first = pltpu.roll(value, x, 1)
        last = pltpu.roll(value, lax.rem(rows + x + 1, cells), 1)
        edges = jnp.where(lane == x, first, edges)
        return jnp.where(lane == rows + x, last, edges)

    edges = lax.fori_loop(0, rows, pack_row, jnp.zeros((full, cells), F32))
    edge_out[...] = edges.astype(BF16)

    def own_row(i, carry):
        arrived[lax.div(i, step), mz, lax.rem(i, step)] = masked[1 + mz * group + i]
        return carry

    lax.fori_loop(0, group, own_row, 0)

    pl.semaphore_wait(barrier, (nx - 1) + (ny - 1) + (nz - 1))

    def forward(c, k):
        to = lax.rem(mz + k, nz)
        return pltpu.make_async_remote_copy(
            src_ref=masked.at[pl.ds(1 + to * group + c * step, step)],
            dst_ref=arrived.at[c, mz],
            send_sem=fs.at[c, to],
            recv_sem=fr.at[c, mz],
            device_id={"lz": to},
            device_id_type=MESH,
        )

    def forward_in(c, k):
        src = lax.rem(mz + nz - k, nz)
        return pltpu.make_async_remote_copy(
            src_ref=arrived.at[c, src],
            dst_ref=arrived.at[c, src],
            send_sem=fs.at[c, src],
            recv_sem=fr.at[c, src],
            device_id={"lz": src},
            device_id_type=MESH,
        )

    def backward(c, k):
        to = lax.rem(mz + k, nz)
        return pltpu.make_async_remote_copy(
            src_ref=product.at[c, to],
            dst_ref=coupled.at[pl.ds(mz * group + c * step, step)],
            send_sem=bs.at[c, to],
            recv_sem=br.at[c, mz],
            device_id={"lz": to},
            device_id_type=MESH,
        )

    def backward_in(c, k):
        src = lax.rem(mz + nz - k, nz)
        return pltpu.make_async_remote_copy(
            src_ref=product.at[c, src],
            dst_ref=coupled.at[pl.ds(src * group + c * step, step)],
            send_sem=bs.at[c, src],
            recv_sem=br.at[c, src],
            device_id={"lz": src},
            device_id_type=MESH,
        )

    order = sorted(range(1, nz), key=lambda k: -min(k, nz - k))
    for k in order:
        forward(0, k).start()
    later, before = lax.rem(mx + 1, nx), lax.rem(mx + nx - 1, nx)
    to_later = pltpu.make_async_remote_copy(
        src_ref=masked.at[rows], dst_ref=masked.at[0], send_sem=xs.at[0], recv_sem=xr.at[0],
        device_id={"tx": later}, device_id_type=MESH,
    )
    to_before = pltpu.make_async_remote_copy(
        src_ref=masked.at[1], dst_ref=masked.at[rows + 1], send_sem=xs.at[1], recv_sem=xr.at[1],
        device_id={"tx": before}, device_id_type=MESH,
    )
    to_later.start()
    to_before.start()
    up, down = lax.rem(my + 1, ny), lax.rem(my + ny - 1, ny)
    to_up = pltpu.make_async_remote_copy(
        src_ref=edge_out, dst_ref=edge_in.at[0], send_sem=ys.at[0], recv_sem=yr.at[0],
        device_id={"ty": up}, device_id_type=MESH,
    )
    to_down = pltpu.make_async_remote_copy(
        src_ref=edge_out, dst_ref=edge_in.at[1], send_sem=ys.at[1], recv_sem=yr.at[1],
        device_id={"ty": down}, device_id_type=MESH,
    )
    to_up.start()
    to_down.start()
    for c in range(1, chunks):
        for k in order:
            forward(c, k).start()

    for f in range(2):
        for u in range(units):
            rates[pl.ds(f * slab + u * layers, layers), :] = jnp.full(
                (layers, cells), kappa_ref[u], F32
            )

    col = units * layers * nz
    wide = nz * full

    def chooser(shape, dim, f):
        i = lax.broadcasted_iota(jnp.int32, shape, dim)
        j = lax.broadcasted_iota(jnp.int32, shape, 1 - dim)
        part, rest = i // full, lax.rem(i, full)
        field, entry = rest // slab, lax.rem(rest, slab)
        unit, layer = entry // layers, lax.rem(entry, layers)
        target = unit * (layers * nz) + part * layers + layer
        return jnp.where((target == j) & (field == f), 1.0, 0.0).astype(BF16)

    dense = k_ref[...]
    total = None
    for f in range(2):
        left = jnp.dot(
            chooser((wide, col), 0, f), dense, preferred_element_type=F32
        ).astype(BF16)
        both = jnp.dot(left, chooser((col, wide), 1, f), preferred_element_type=F32)
        total = both if total is None else total + both
    big_k[...] = total.astype(BF16)

    zero = jnp.zeros((layers, cells), F32)
    sums = (zero, zero, zero)

    def norms(x, carry):
        bb, cc, cv = carry
        for u in range(units):
            b = b_ref[x, u].astype(F32)
            c = c_ref[x, u].astype(F32)
            bb = bb + b * b
            cc = cc + c * c
            cv = cv + c * test_ref[x, u].astype(F32)
        return bb, cc, cv

    quarter = rows // chunks
    for c in range(chunks):
        for k in order:
            forward_in(c, k).wait_recv()
        part = jnp.concatenate(
            [arrived[c, :, r].reshape(wide, cells) for r in range(step)], axis=1
        )
        result = jnp.dot(big_k[...], part, preferred_element_type=F32).astype(BF16)
        for d in range(nz):
            for r in range(step):
                product[c, d, r] = result[d * full:(d + 1) * full, r * cells:(r + 1) * cells]
        sums = lax.fori_loop(c * quarter, (c + 1) * quarter, norms, sums)
        for k in order:
            backward(c, k).start()
        for r in range(step):
            coupled[mz * group + c * step + r] = product[c, mz, r]

    to_later.wait_recv()
    to_before.wait_recv()
    to_up.wait_recv()
    to_down.wait_recv()

    @pl.when(my > 0)
    def _():
        edge_f[0] = edge_in[0].astype(F32)

    @pl.when(my == 0)
    def _():
        edge_f[0] = jnp.zeros((full, cells), F32)

    @pl.when(my < ny - 1)
    def _():
        edge_f[1] = edge_in[1].astype(F32)

    @pl.when(my == ny - 1)
    def _():
        edge_f[1] = jnp.zeros((full, cells), F32)

    def image_row(x, carry):
        ba, be = carry
        here = masked[x + 1].astype(F32)
        south = jnp.where(
            lane == 0, pltpu.roll(edge_f[0], lax.rem(2 * cells - rows - x, cells), 1),
            pltpu.roll(here, 1, 1),
        )
        north = jnp.where(
            lane == cells - 1, pltpu.roll(edge_f[1], cells - 1 - x, 1),
            pltpu.roll(here, cells - 1, 1),
        )
        near = masked[x].astype(F32) + masked[x + 2].astype(F32) + south + north - 4.0 * here
        spread_s[...] = coupled[x].astype(F32) + rates[...] * near
        blocks_s[...] = blocks_ref[x].astype(F32)
        row = weight[pl.ds(x, 1), :]
        source = [[fields[f][x, w].astype(F32) * row for w in range(units)] for f in range(2)]
        for u in range(units):
            mix = [blocks_s[pl.ds(units * u + w, 1), :] for w in range(units)]
            b = b_ref[x, u].astype(F32)
            images = []
            for f in range(2):
                value = spread_s[pl.ds(f * slab + u * layers, layers), :]
                for w in range(units):
                    value = value + mix[w] * source[f][w]
                images.append(row * value)
            out_t[x, u] = images[0].astype(BF16)
            out_d[x, u] = images[1].astype(BF16)
            ba = ba + b * images[0]
            be = be + b * images[1]
        return ba, be

    pair = (zero, zero)
    for c in range(chunks):
        for k in order:
            backward_in(c, k).wait_recv()

        def chunk_row(i, carry):
            x = lax.div(i, step) * group + c * step + lax.rem(i, step)
            return image_row(x, carry)

        pair = lax.fori_loop(0, nz * step, chunk_row, pair)

    lines = [jnp.sum(v, axis=0, keepdims=True) for v in (*sums, *pair)]
    value = jnp.concatenate(lines + [jnp.zeros((3, cells), F32)], axis=0)
    base = 0
    stages = (
        ("lz", mz, nz, stat_z, sr_z), ("ty", my, ny, stat_y, sr_y), ("tx", mx, nx, stat_x, sr_x)
    )
    sends = []
    for s, (name, me, size, box, sem) in enumerate(stages):
        stat_out[s] = value
        box[me] = value
        for k in range(1, size):
            copy = pltpu.make_async_remote_copy(
                src_ref=stat_out.at[s], dst_ref=box.at[me], send_sem=ss.at[base + k - 1],
                recv_sem=sem.at[me], device_id={name: lax.rem(me + k, size)},
                device_id_type=MESH,
            )
            copy.start()
            sends.append(copy)
        base += size - 1
        for k in range(1, size):
            src = lax.rem(me + size - k, size)
            pltpu.make_async_remote_copy(
                src_ref=stat_out.at[s], dst_ref=box.at[src], send_sem=ss.at[0],
                recv_sem=sem.at[src], device_id={name: src}, device_id_type=MESH,
            ).wait_recv()
        value = box[0]
        for i in range(1, size):
            value = value + box[i]
    final = jnp.broadcast_to(jnp.sum(value, axis=1, keepdims=True), (8, cells))
    bb, cc, cv, ba, be = (final[i:i + 1] for i in range(5))
    line = lax.broadcasted_iota(jnp.int32, (1, cells), 1)
    top = jnp.where(line == 0, ba, jnp.where(line == 1, be, cv))
    low = jnp.where(line == 2, cc, bb)
    border_ref[...] = top / jnp.sqrt(low)

    for c in range(chunks):
        for k in order:
            forward(c, k).wait_send()
            backward(c, k).wait_send()
    to_later.wait_send()
    to_before.wait_send()
    to_up.wait_send()
    to_down.wait_send()
    for copy in sends:
        copy.wait_send()


def body(sizes, *arrays):
    test_field = arrays[0]
    nx, ny, nz = sizes
    rows, units, layers, cells = test_field.shape
    full = 2 * units * layers
    group = rows // nz
    chunks = 4 if group % 4 == 0 else 1
    step = group // chunks
    mixes = arrays[6].shape[1]
    vmem = pl.BlockSpec(memory_space=pltpu.VMEM)
    smem = pl.BlockSpec(memory_space=pltpu.SMEM)
    dma = pltpu.SemaphoreType.DMA
    out_t, out_d, border = pl.pallas_call(
        functools.partial(kernel, sizes, chunks),
        out_shape=(
            jax.ShapeDtypeStruct(test_field.shape, BF16),
            jax.ShapeDtypeStruct(test_field.shape, BF16),
            jax.ShapeDtypeStruct((1, cells), F32),
        ),
        in_specs=[vmem] * 8 + [smem],
        out_specs=(vmem, vmem, vmem),
        scratch_shapes=[
            pltpu.VMEM((rows + 2, full, cells), BF16),
            pltpu.VMEM((chunks, nz, step, full, cells), BF16),
            pltpu.VMEM((chunks, nz, step, full, cells), BF16),
            pltpu.VMEM((rows, full, cells), BF16),
            pltpu.VMEM((rows, cells), F32),
            pltpu.VMEM((full, cells), F32),
            pltpu.VMEM((nz * full, nz * full), BF16),
            pltpu.VMEM((full, cells), F32),
            pltpu.VMEM((full, cells), F32),
            pltpu.VMEM((mixes, cells), F32),
            pltpu.VMEM((full, cells), BF16),
            pltpu.VMEM((2, full, cells), BF16),
            pltpu.VMEM((2, full, cells), F32),
            pltpu.VMEM((3, 8, cells), F32),
            pltpu.VMEM((nz, 8, cells), F32),
            pltpu.VMEM((ny, 8, cells), F32),
            pltpu.VMEM((nx, 8, cells), F32),
            dma((chunks, nz)),
            dma((chunks, nz)),
            dma((chunks, nz)),
            dma((chunks, nz)),
            dma((2,)),
            dma((2,)),
            dma((2,)),
            dma((2,)),
            dma((nx + ny + nz - 3,)),
            dma((nz,)),
            dma((ny,)),
            dma((nx,)),
        ],
        compiler_params=pltpu.CompilerParams(
            collective_id=0, has_side_effects=True, vmem_limit_bytes=48 * 1024 * 1024
        ),
    )(*arrays)
    return out_t, out_d, border[0, :3]


def solution(mesh):
    wide = P("tx", None, "lz", "ty")
    in_specs = (
        wide, wide, wide, wide, P("tx", "ty"), P("tx", "ty"), P("tx", None, "ty"), P(), P(),
    )
    sizes = tuple(mesh.shape[name] for name in ("tx", "ty", "lz"))
    return jax.shard_map(
        functools.partial(body, sizes), mesh=mesh, in_specs=in_specs,
        out_specs=(wide, wide, P()), check_vma=False,
    )
```

```python
import functools
import jax
import jax.numpy as jnp
from jax import lax
from jax.experimental import pallas as pl
from jax.experimental.pallas import tpu as pltpu
from jax.sharding import PartitionSpec as P

MESH = pl.DeviceIdType.MESH
F32 = jnp.float32
BF16 = jnp.bfloat16


MARGIN = 8


def kernel(
    sizes, chunks, units,
    test_hbm, dir_hbm, b_hbm, c_hbm, land_ref, active_ref, blocks_hbm, k_hbm, kappa_ref,
    out_t, out_d, border_ref,
    test_ref, dir_ref, b_ref, c_ref, blocks_ref, k_ref,
    masked, arrived, product, coupled, weight, big_k, field, back, before_image, halo,
    edge_out, edge_in, edge_f, stat_out, stat_z, stat_y, stat_x,
    ls, fs, fr, bs, br, xs, xr, ys, yr, ss, sr_z, sr_y, sr_x,
):
    nx, ny, nz = sizes
    slab, rows, cells = test_ref.shape
    layers = slab // units
    full = 2 * slab
    group = rows // nz
    step = group // chunks
    pitch = rows + 2 * MARGIN
    mx, my, mz = lax.axis_index("tx"), lax.axis_index("ty"), lax.axis_index("lz")
    fields = (test_ref, dir_ref)
    outs = (out_t, out_d)

    loads = [
        pltpu.make_async_copy(source, target, ls.at[i])
        for i, (source, target) in enumerate((
            (test_hbm, test_ref), (dir_hbm, dir_ref), (k_hbm, k_ref), (b_hbm, b_ref),
            (c_hbm, c_ref), (blocks_hbm, blocks_ref),
        ))
    ]
    for load in loads:
        load.start()

    barrier = pltpu.get_barrier_semaphore()
    for name, me, size in (("tx", mx, nx), ("ty", my, ny), ("lz", mz, nz)):
        for k in range(1, size):
            pl.semaphore_signal(
                barrier, inc=1, device_id={name: lax.rem(me + k, size)}, device_id_type=MESH
            )

    lane = lax.broadcasted_iota(jnp.int32, (rows, cells), 1)
    line = lax.broadcasted_iota(jnp.int32, (rows, rows), 0)
    named = jnp.max(
        jnp.where(jnp.broadcast_to(active_ref[...], (rows, rows)) == line, 1.0, 0.0),
        axis=1, keepdims=True,
    )
    weight[...] = land_ref[...].astype(F32) * named
    ocean = weight[...]

    def middle(q):
        return pl.ds(pl.multiple_of(q * pitch + MARGIN, 8), rows)

    for f in range(2):
        loads[f].wait()

        def mask(j, edges):
            first, last = edges
            value = fields[f][j].astype(F32) * ocean
            field[middle(f * slab + j), :] = value
            first = jnp.where(lane == j, pltpu.roll(value, j, 1), first)
            last = jnp.where(lane == j, pltpu.roll(value, j + 1, 1), last)
            return first, last

        blank = jnp.zeros((rows, cells), F32)
        first, last = lax.fori_loop(0, slab, mask, (blank, blank), unroll=2)
        edge_out[0, f] = first.astype(BF16)
        edge_out[1, f] = last.astype(BF16)

    def pack(x, carry):
        masked[x] = field[pl.ds(MARGIN + x, full, stride=pitch), :].astype(BF16)
        return carry

    lax.fori_loop(0, rows, pack, 0, unroll=2)

    def own_row(i, carry):
        arrived[lax.div(i, step), mz, lax.rem(i, step)] = masked[mz * group + i]
        return carry

    lax.fori_loop(0, group, own_row, 0)

    pl.semaphore_wait(barrier, (nx - 1) + (ny - 1) + (nz - 1))

    def forward(c, k):
        to = lax.rem(mz + k, nz)
        return pltpu.make_async_remote_copy(
            src_ref=masked.at[pl.ds(to * group + c * step, step)],
            dst_ref=arrived.at[c, mz],
            send_sem=fs.at[c, to],
            recv_sem=fr.at[c, mz],
            device_id={"lz": to},
            device_id_type=MESH,
        )

    def forward_in(c, k):
        src = lax.rem(mz + nz - k, nz)
        return pltpu.make_async_remote_copy(
            src_ref=arrived.at[c, src],
            dst_ref=arrived.at[c, src],
            send_sem=fs.at[c, src],
            recv_sem=fr.at[c, src],
            device_id={"lz": src},
            device_id_type=MESH,
        )

    def backward(c, k):
        to = lax.rem(mz + k, nz)
        return pltpu.make_async_remote_copy(
            src_ref=product.at[c, to],
            dst_ref=coupled.at[pl.ds(mz * group + c * step, step)],
            send_sem=bs.at[c, to],
            recv_sem=br.at[c, mz],
            device_id={"lz": to},
            device_id_type=MESH,
        )

    def backward_in(c, k):
        src = lax.rem(mz + nz - k, nz)
        return pltpu.make_async_remote_copy(
            src_ref=product.at[c, src],
            dst_ref=coupled.at[pl.ds(src * group + c * step, step)],
            send_sem=bs.at[c, src],
            recv_sem=br.at[c, src],
            device_id={"lz": src},
            device_id_type=MESH,
        )

    order = sorted(range(1, nz), key=lambda k: -min(k, nz - k))
    for k in order:
        forward(0, k).start()
    later, before = lax.rem(mx + 1, nx), lax.rem(mx + nx - 1, nx)
    to_later = pltpu.make_async_remote_copy(
        src_ref=masked.at[rows - 1], dst_ref=halo.at[0], send_sem=xs.at[0], recv_sem=xr.at[0],
        device_id={"tx": later}, device_id_type=MESH,
    )
    to_before = pltpu.make_async_remote_copy(
        src_ref=masked.at[0], dst_ref=halo.at[1], send_sem=xs.at[1], recv_sem=xr.at[1],
        device_id={"tx": before}, device_id_type=MESH,
    )
    to_later.start()
    to_before.start()
    up, down = lax.rem(my + 1, ny), lax.rem(my + ny - 1, ny)
    to_up = pltpu.make_async_remote_copy(
        src_ref=edge_out.at[1], dst_ref=edge_in.at[0], send_sem=ys.at[0], recv_sem=yr.at[0],
        device_id={"ty": up}, device_id_type=MESH,
    )
    to_down = pltpu.make_async_remote_copy(
        src_ref=edge_out.at[0], dst_ref=edge_in.at[1], send_sem=ys.at[1], recv_sem=yr.at[1],
        device_id={"ty": down}, device_id_type=MESH,
    )
    to_up.start()
    to_down.start()
    for c in range(1, chunks):
        for k in order:
            forward(c, k).start()

    col = units * layers * nz
    wide = nz * full

    def chooser(shape, dim, f):
        i = lax.broadcasted_iota(jnp.int32, shape, dim)
        j = lax.broadcasted_iota(jnp.int32, shape, 1 - dim)
        part, rest = i // full, lax.rem(i, full)
        field, entry = rest // slab, lax.rem(rest, slab)
        unit, layer = entry // layers, lax.rem(entry, layers)
        target = unit * (layers * nz) + part * layers + layer
        return jnp.where((target == j) & (field == f), 1.0, 0.0).astype(BF16)

    loads[2].wait()
    dense = k_ref[...]
    total = None
    for f in range(2):
        left = jnp.dot(
            chooser((wide, col), 0, f), dense, preferred_element_type=F32
        ).astype(BF16)
        both = jnp.dot(left, chooser((col, wide), 1, f), preferred_element_type=F32)
        total = both if total is None else total + both
    big_k[...] = total.astype(BF16)

    for load in loads[3:]:
        load.wait()
    zero = jnp.zeros((rows, cells), F32)
    sums = (zero, zero, zero)

    def norms(j, carry):
        bb, cc, cv = carry
        b = b_ref[j].astype(F32)
        c = c_ref[j].astype(F32)
        return bb + b * b, cc + c * c, cv + c * test_ref[j].astype(F32)

    quarter = slab // chunks
    for c in range(chunks):
        for k in order:
            forward_in(c, k).wait_recv()
        part = jnp.concatenate(
            [arrived[c, :, r].reshape(wide, cells) for r in range(step)], axis=1
        )
        result = jnp.dot(big_k[...], part, preferred_element_type=F32).astype(BF16)
        for d in range(nz):
            for r in range(step):
                product[c, d, r] = result[d * full:(d + 1) * full, r * cells:(r + 1) * cells]
        sums = lax.fori_loop(c * quarter, (c + 1) * quarter, norms, sums)
        for k in order:
            backward(c, k).start()
        for r in range(step):
            coupled[mz * group + c * step + r] = product[c, mz, r]

    to_later.wait_recv()
    to_before.wait_recv()
    to_up.wait_recv()
    to_down.wait_recv()
    field[pl.ds(MARGIN - 1, full, stride=pitch), :] = halo[0].astype(F32)
    field[pl.ds(MARGIN + rows, full, stride=pitch), :] = halo[1].astype(F32)

    @pl.when(my > 0)
    def _():
        edge_f[0] = edge_in[0].astype(F32)

    @pl.when(my == 0)
    def _():
        edge_f[0] = jnp.zeros((2, rows, cells), F32)

    @pl.when(my < ny - 1)
    def _():
        edge_f[1] = edge_in[1].astype(F32)

    @pl.when(my == ny - 1)
    def _():
        edge_f[1] = jnp.zeros((2, rows, cells), F32)

    for f in range(2):
        for u in range(units):
            def local(z, carry):
                j = u * layers + z
                q = f * slab + j
                here = field[middle(q), :]
                south = jnp.where(
                    lane == 0, pltpu.roll(edge_f[0, f], lax.rem(cells - j, cells), 1),
                    pltpu.roll(here, 1, 1),
                )
                north = jnp.where(
                    lane == cells - 1, pltpu.roll(edge_f[1, f], cells - 1 - j, 1),
                    pltpu.roll(here, cells - 1, 1),
                )
                near = field[pl.ds(q * pitch + MARGIN - 1, rows), :]
                near = near + field[pl.ds(q * pitch + MARGIN + 1, rows), :]
                value = kappa_ref[u] * (near + south + north - 4.0 * here)
                for w in range(units):
                    value = value + blocks_ref[units * u + w].astype(F32) * field[
                        middle(f * slab + w * layers + z), :
                    ]
                before_image[q] = value
                return carry

            lax.fori_loop(0, layers, local, 0)

    def insert(x, carry):
        back[pl.ds(x, full, stride=rows), :] = coupled[x].astype(F32)
        return carry

    for c in range(chunks):
        for k in order:
            backward_in(c, k).wait_recv()

        def chunk_row(i, carry):
            return insert(lax.div(i, step) * group + c * step + lax.rem(i, step), carry)

        lax.fori_loop(0, nz * step, chunk_row, 0, unroll=2)

    def image(j, carry):
        ba, be = carry
        b = b_ref[j].astype(F32)
        images = []
        for f in range(2):
            q = f * slab + j
            coup = back[pl.ds(pl.multiple_of(q * rows, 8), rows), :]
            images.append(ocean * (coup + before_image[q]))
            outs[f][j] = images[f].astype(BF16)
        return ba + b * images[0], be + b * images[1]

    pair = lax.fori_loop(0, slab, image, (zero, zero), unroll=2)

    lines = [jnp.sum(v, axis=0, keepdims=True) for v in (*sums, *pair)]
    value = jnp.concatenate(lines + [jnp.zeros((3, cells), F32)], axis=0)
    base = 0
    stages = (
        ("lz", mz, nz, stat_z, sr_z), ("ty", my, ny, stat_y, sr_y), ("tx", mx, nx, stat_x, sr_x)
    )
    sends = []
    for s, (name, me, size, box, sem) in enumerate(stages):
        stat_out[s] = value
        box[me] = value
        for k in range(1, size):
            copy = pltpu.make_async_remote_copy(
                src_ref=stat_out.at[s], dst_ref=box.at[me], send_sem=ss.at[base + k - 1],
                recv_sem=sem.at[me], device_id={name: lax.rem(me + k, size)},
                device_id_type=MESH,
            )
            copy.start()
            sends.append(copy)
        base += size - 1
        for k in range(1, size):
            src = lax.rem(me + size - k, size)
            pltpu.make_async_remote_copy(
                src_ref=stat_out.at[s], dst_ref=box.at[src], send_sem=ss.at[0],
                recv_sem=sem.at[src], device_id={name: src}, device_id_type=MESH,
            ).wait_recv()
        value = box[0]
        for i in range(1, size):
            value = value + box[i]
    final = jnp.broadcast_to(jnp.sum(value, axis=1, keepdims=True), (8, cells))
    bb, cc, cv, ba, be = (final[i:i + 1] for i in range(5))
    line = lax.broadcasted_iota(jnp.int32, (1, cells), 1)
    top = jnp.where(line == 0, ba, jnp.where(line == 1, be, cv))
    low = jnp.where(line == 2, cc, bb)
    border_ref[...] = top / jnp.sqrt(low)

    for c in range(chunks):
        for k in order:
            forward(c, k).wait_send()
            backward(c, k).wait_send()
    to_later.wait_send()
    to_before.wait_send()
    to_up.wait_send()
    to_down.wait_send()
    for copy in sends:
        copy.wait_send()


def body(sizes, *arrays):
    nx, ny, nz = sizes
    rows, units, layers, cells = arrays[0].shape
    slab = units * layers
    full = 2 * slab
    group = rows // nz
    chunks = 4 if group % 4 == 0 else 1
    step = group // chunks
    mixes = arrays[6].shape[1]
    wide = [v.transpose(1, 2, 0, 3).reshape(slab, rows, cells) for v in arrays[:4]]
    args = (*wide, arrays[4], arrays[5].T, arrays[6].transpose(1, 0, 2), *arrays[7:])
    vmem = pl.BlockSpec(memory_space=pltpu.VMEM)
    smem = pl.BlockSpec(memory_space=pltpu.SMEM)
    hbm = pl.BlockSpec(memory_space=pl.ANY)
    dma = pltpu.SemaphoreType.DMA
    out_t, out_d, border = pl.pallas_call(
        functools.partial(kernel, sizes, chunks, units),
        out_shape=(
            jax.ShapeDtypeStruct((slab, rows, cells), BF16),
            jax.ShapeDtypeStruct((slab, rows, cells), BF16),
            jax.ShapeDtypeStruct((1, cells), F32),
        ),
        in_specs=[hbm] * 4 + [vmem] * 2 + [hbm] * 2 + [smem],
        out_specs=(vmem, vmem, vmem),
        scratch_shapes=[
            *[pltpu.VMEM((slab, rows, cells), BF16)] * 4,
            pltpu.VMEM((mixes, rows, cells), BF16),
            pltpu.VMEM(arrays[7].shape, BF16),
            pltpu.VMEM((rows, full, cells), BF16),
            pltpu.VMEM((chunks, nz, step, full, cells), BF16),
            pltpu.VMEM((chunks, nz, step, full, cells), BF16),
            pltpu.VMEM((rows, full, cells), BF16),
            pltpu.VMEM((rows, cells), F32),
            pltpu.VMEM((nz * full, nz * full), BF16),
            pltpu.VMEM((full * (rows + 2 * MARGIN), cells), F32),
            pltpu.VMEM((full * rows, cells), F32),
            pltpu.VMEM((full, rows, cells), F32),
            pltpu.VMEM((2, full, cells), BF16),
            pltpu.VMEM((2, 2, rows, cells), BF16),
            pltpu.VMEM((2, 2, rows, cells), BF16),
            pltpu.VMEM((2, 2, rows, cells), F32),
            pltpu.VMEM((3, 8, cells), F32),
            pltpu.VMEM((nz, 8, cells), F32),
            pltpu.VMEM((ny, 8, cells), F32),
            pltpu.VMEM((nx, 8, cells), F32),
            dma((6,)),
            dma((chunks, nz)),
            dma((chunks, nz)),
            dma((chunks, nz)),
            dma((chunks, nz)),
            dma((2,)),
            dma((2,)),
            dma((2,)),
            dma((2,)),
            dma((nx + ny + nz - 3,)),
            dma((nz,)),
            dma((ny,)),
            dma((nx,)),
        ],
        compiler_params=pltpu.CompilerParams(
            collective_id=0, has_side_effects=True, vmem_limit_bytes=56 * 1024 * 1024
        ),
    )(*args)
    outs = [
        v.reshape(units, layers, rows, cells).transpose(2, 0, 1, 3) for v in (out_t, out_d)
    ]
    return (*outs, border[0, :3])


def solution(mesh):
    wide = P("tx", None, "lz", "ty")
    in_specs = (
        wide, wide, wide, wide, P("tx", "ty"), P("tx", "ty"), P("tx", None, "ty"), P(), P(),
    )
    sizes = tuple(mesh.shape[name] for name in ("tx", "ty", "lz"))
    return jax.shard_map(
        functools.partial(body, sizes), mesh=mesh, in_specs=in_specs,
        out_specs=(wide, wide, P()), check_vma=False,
    )
```

```python
import functools
import jax
import jax.numpy as jnp
from jax import lax
from jax.experimental import pallas as pl
from jax.experimental.pallas import tpu as pltpu
from jax.sharding import PartitionSpec as P

MESH = pl.DeviceIdType.MESH
F32 = jnp.float32
BF16 = jnp.bfloat16


MARGIN = 8


def kernel(
    sizes, chunks, units,
    test_hbm, dir_hbm, b_hbm, c_hbm, land_ref, active_ref, blocks_hbm, k_hbm, kappa_ref,
    out_t, out_d, border_ref,
    test_ref, dir_ref, b_ref, c_ref, blocks_ref, k_ref,
    masked, arrived, product, coupled, weight, big_k, field, back, before_image, halo,
    edge_out, edge_in, edge_f, stat_out, stat_z, stat_y, stat_x,
    ls, fs, fr, bs, br, xs, xr, ys, yr, ss, sr_z, sr_y, sr_x,
):
    nx, ny, nz = sizes
    slab, rows, cells = test_ref.shape
    layers = slab // units
    full = 2 * slab
    group = rows // nz
    step = group // chunks
    pitch = rows + 2 * MARGIN
    mx, my, mz = lax.axis_index("tx"), lax.axis_index("ty"), lax.axis_index("lz")
    fields = (test_ref, dir_ref)
    outs = (out_t, out_d)

    loads = [
        pltpu.make_async_copy(source, target, ls.at[i])
        for i, (source, target) in enumerate((
            (test_hbm, test_ref), (dir_hbm, dir_ref), (k_hbm, k_ref), (b_hbm, b_ref),
            (c_hbm, c_ref), (blocks_hbm, blocks_ref),
        ))
    ]
    for load in loads:
        load.start()

    barrier = pltpu.get_barrier_semaphore()
    for name, me, size in (("tx", mx, nx), ("ty", my, ny), ("lz", mz, nz)):
        for k in range(1, size):
            pl.semaphore_signal(
                barrier, inc=1, device_id={name: lax.rem(me + k, size)}, device_id_type=MESH
            )

    lane = lax.broadcasted_iota(jnp.int32, (rows, cells), 1)
    line = lax.broadcasted_iota(jnp.int32, (rows, rows), 0)
    named = jnp.max(
        jnp.where(jnp.broadcast_to(active_ref[...], (rows, rows)) == line, 1.0, 0.0),
        axis=1, keepdims=True,
    )
    weight[...] = land_ref[...].astype(F32) * named
    ocean = weight[...]

    def middle(q):
        return pl.ds(pl.multiple_of(q * pitch + MARGIN, 8), rows)

    for f in range(2):
        loads[f].wait()

        def mask(j, carry):
            field[middle(f * slab + j), :] = fields[f][j].astype(F32) * ocean
            return carry

        lax.fori_loop(0, slab, mask, 0, unroll=8)

    def pack(c):
        def pack_row(i, carry):
            x = lax.div(i, step) * group + c * step + lax.rem(i, step)
            masked[x] = field[pl.ds(MARGIN + x, full, stride=pitch), :].astype(BF16)
            return carry

        lax.fori_loop(0, nz * step, pack_row, 0, unroll=4)

    pack(0)

    pl.semaphore_wait(barrier, (nx - 1) + (ny - 1) + (nz - 1))

    def forward(c, k):
        to = lax.rem(mz + k, nz)
        return pltpu.make_async_remote_copy(
            src_ref=masked.at[pl.ds(to * group + c * step, step)],
            dst_ref=arrived.at[c, mz],
            send_sem=fs.at[c, to],
            recv_sem=fr.at[c, mz],
            device_id={"lz": to},
            device_id_type=MESH,
        )

    def forward_in(c, k):
        src = lax.rem(mz + nz - k, nz)
        return pltpu.make_async_remote_copy(
            src_ref=arrived.at[c, src],
            dst_ref=arrived.at[c, src],
            send_sem=fs.at[c, src],
            recv_sem=fr.at[c, src],
            device_id={"lz": src},
            device_id_type=MESH,
        )

    def backward(c, k):
        to = lax.rem(mz + k, nz)
        return pltpu.make_async_remote_copy(
            src_ref=product.at[c, to],
            dst_ref=coupled.at[pl.ds(mz * group + c * step, step)],
            send_sem=bs.at[c, to],
            recv_sem=br.at[c, mz],
            device_id={"lz": to},
            device_id_type=MESH,
        )

    def backward_in(c, k):
        src = lax.rem(mz + nz - k, nz)
        return pltpu.make_async_remote_copy(
            src_ref=product.at[c, src],
            dst_ref=coupled.at[pl.ds(src * group + c * step, step)],
            send_sem=bs.at[c, src],
            recv_sem=br.at[c, src],
            device_id={"lz": src},
            device_id_type=MESH,
        )

    order = sorted(range(1, nz), key=lambda k: -min(k, nz - k))
    for c in range(1, chunks):
        pack(c)
        for k in order:
            forward(c - 1, k).start()

    def own_row(i, carry):
        arrived[lax.div(i, step), mz, lax.rem(i, step)] = masked[mz * group + i]
        return carry

    lax.fori_loop(0, group, own_row, 0)
    for k in order:
        forward(chunks - 1, k).start()
    later, before = lax.rem(mx + 1, nx), lax.rem(mx + nx - 1, nx)
    to_later = pltpu.make_async_remote_copy(
        src_ref=masked.at[rows - 1], dst_ref=halo.at[0], send_sem=xs.at[0], recv_sem=xr.at[0],
        device_id={"tx": later}, device_id_type=MESH,
    )
    to_before = pltpu.make_async_remote_copy(
        src_ref=masked.at[0], dst_ref=halo.at[1], send_sem=xs.at[1], recv_sem=xr.at[1],
        device_id={"tx": before}, device_id_type=MESH,
    )
    to_later.start()
    to_before.start()
    for f in range(2):
        def edges(j, carry):
            first, last = carry
            value = field[middle(f * slab + j), :]
            first = jnp.where(lane == j, pltpu.roll(value, j, 1), first)
            last = jnp.where(lane == j, pltpu.roll(value, j + 1, 1), last)
            return first, last

        blank = jnp.zeros((rows, cells), F32)
        first, last = lax.fori_loop(0, slab, edges, (blank, blank), unroll=4)
        edge_out[0, f] = first.astype(BF16)
        edge_out[1, f] = last.astype(BF16)

    up, down = lax.rem(my + 1, ny), lax.rem(my + ny - 1, ny)
    to_up = pltpu.make_async_remote_copy(
        src_ref=edge_out.at[1], dst_ref=edge_in.at[0], send_sem=ys.at[0], recv_sem=yr.at[0],
        device_id={"ty": up}, device_id_type=MESH,
    )
    to_down = pltpu.make_async_remote_copy(
        src_ref=edge_out.at[0], dst_ref=edge_in.at[1], send_sem=ys.at[1], recv_sem=yr.at[1],
        device_id={"ty": down}, device_id_type=MESH,
    )
    col = units * layers * nz
    wide = nz * full

    def chooser(shape, dim, f):
        i = lax.broadcasted_iota(jnp.int32, shape, dim)
        j = lax.broadcasted_iota(jnp.int32, shape, 1 - dim)
        part, rest = i // full, lax.rem(i, full)
        field, entry = rest // slab, lax.rem(rest, slab)
        unit, layer = entry // layers, lax.rem(entry, layers)
        target = unit * (layers * nz) + part * layers + layer
        return jnp.where((target == j) & (field == f), 1.0, 0.0).astype(BF16)

    loads[2].wait()
    dense = k_ref[...]
    total = None
    for f in range(2):
        left = jnp.dot(
            chooser((wide, col), 0, f), dense, preferred_element_type=F32
        ).astype(BF16)
        both = jnp.dot(left, chooser((col, wide), 1, f), preferred_element_type=F32)
        total = both if total is None else total + both
    big_k[...] = total.astype(BF16)
    to_up.start()
    to_down.start()

    for load in loads[3:]:
        load.wait()
    zero = jnp.zeros((rows, cells), F32)
    sums = (zero, zero, zero)

    def norms(j, carry):
        bb, cc, cv = carry
        b = b_ref[j].astype(F32)
        c = c_ref[j].astype(F32)
        return bb + b * b, cc + c * c, cv + c * test_ref[j].astype(F32)

    quarter = slab // chunks
    for c in range(chunks):
        for k in order:
            forward_in(c, k).wait_recv()
        part = jnp.concatenate(
            [arrived[c, :, r].reshape(wide, cells) for r in range(step)], axis=1
        )
        result = jnp.dot(big_k[...], part, preferred_element_type=F32).astype(BF16)
        for d in range(nz):
            for r in range(step):
                product[c, d, r] = result[d * full:(d + 1) * full, r * cells:(r + 1) * cells]
        sums = lax.fori_loop(c * quarter, (c + 1) * quarter, norms, sums, unroll=2)
        for k in order:
            backward(c, k).start()
        for r in range(step):
            coupled[mz * group + c * step + r] = product[c, mz, r]

    to_later.wait_recv()
    to_before.wait_recv()
    to_up.wait_recv()
    to_down.wait_recv()
    field[pl.ds(MARGIN - 1, full, stride=pitch), :] = halo[0].astype(F32)
    field[pl.ds(MARGIN + rows, full, stride=pitch), :] = halo[1].astype(F32)

    @pl.when(my > 0)
    def _():
        edge_f[0] = edge_in[0].astype(F32)

    @pl.when(my == 0)
    def _():
        edge_f[0] = jnp.zeros((2, rows, cells), F32)

    @pl.when(my < ny - 1)
    def _():
        edge_f[1] = edge_in[1].astype(F32)

    @pl.when(my == ny - 1)
    def _():
        edge_f[1] = jnp.zeros((2, rows, cells), F32)

    for f in range(2):
        for u in range(units):
            def local(z, carry):
                j = u * layers + z
                q = f * slab + j
                here = field[middle(q), :]
                south = jnp.where(
                    lane == 0, pltpu.roll(edge_f[0, f], lax.rem(cells - j, cells), 1),
                    pltpu.roll(here, 1, 1),
                )
                north = jnp.where(
                    lane == cells - 1, pltpu.roll(edge_f[1, f], cells - 1 - j, 1),
                    pltpu.roll(here, cells - 1, 1),
                )
                near = field[pl.ds(q * pitch + MARGIN - 1, rows), :]
                near = near + field[pl.ds(q * pitch + MARGIN + 1, rows), :]
                value = kappa_ref[u] * (near + south + north - 4.0 * here)
                for w in range(units):
                    value = value + blocks_ref[units * u + w].astype(F32) * field[
                        middle(f * slab + w * layers + z), :
                    ]
                before_image[q] = value
                return carry

            lax.fori_loop(0, layers, local, 0, unroll=2)

    def insert(x, carry):
        back[pl.ds(x, full, stride=rows), :] = coupled[x].astype(F32)
        return carry

    for c in range(chunks):
        for k in order:
            backward_in(c, k).wait_recv()

        def chunk_row(i, carry):
            return insert(lax.div(i, step) * group + c * step + lax.rem(i, step), carry)

        lax.fori_loop(0, nz * step, chunk_row, 0, unroll=4)

    def image(j, carry):
        ba, be = carry
        b = b_ref[j].astype(F32)
        images = []
        for f in range(2):
            q = f * slab + j
            coup = back[pl.ds(pl.multiple_of(q * rows, 8), rows), :]
            images.append(ocean * (coup + before_image[q]))
            outs[f][j] = images[f].astype(BF16)
        return ba + b * images[0], be + b * images[1]

    pair = lax.fori_loop(0, slab, image, (zero, zero), unroll=6)

    lines = [jnp.sum(v, axis=0, keepdims=True) for v in (*sums, *pair)]
    value = jnp.concatenate(lines + [jnp.zeros((3, cells), F32)], axis=0)
    base = 0
    stages = (
        ("lz", mz, nz, stat_z, sr_z), ("ty", my, ny, stat_y, sr_y), ("tx", mx, nx, stat_x, sr_x)
    )
    sends = []
    for s, (name, me, size, box, sem) in enumerate(stages):
        stat_out[s] = value
        box[me] = value
        for k in range(1, size):
            copy = pltpu.make_async_remote_copy(
                src_ref=stat_out.at[s], dst_ref=box.at[me], send_sem=ss.at[base + k - 1],
                recv_sem=sem.at[me], device_id={name: lax.rem(me + k, size)},
                device_id_type=MESH,
            )
            copy.start()
            sends.append(copy)
        base += size - 1
        for k in range(1, size):
            src = lax.rem(me + size - k, size)
            pltpu.make_async_remote_copy(
                src_ref=stat_out.at[s], dst_ref=box.at[src], send_sem=ss.at[0],
                recv_sem=sem.at[src], device_id={name: src}, device_id_type=MESH,
            ).wait_recv()
        value = box[0]
        for i in range(1, size):
            value = value + box[i]
    final = jnp.broadcast_to(jnp.sum(value, axis=1, keepdims=True), (8, cells))
    bb, cc, cv, ba, be = (final[i:i + 1] for i in range(5))
    line = lax.broadcasted_iota(jnp.int32, (1, cells), 1)
    top = jnp.where(line == 0, ba, jnp.where(line == 1, be, cv))
    low = jnp.where(line == 2, cc, bb)
    border_ref[...] = top / jnp.sqrt(low)

    for c in range(chunks):
        for k in order:
            forward(c, k).wait_send()
            backward(c, k).wait_send()
    to_later.wait_send()
    to_before.wait_send()
    to_up.wait_send()
    to_down.wait_send()
    for copy in sends:
        copy.wait_send()


def body(sizes, *arrays):
    nx, ny, nz = sizes
    rows, units, layers, cells = arrays[0].shape
    slab = units * layers
    full = 2 * slab
    group = rows // nz
    chunks = 4 if group % 4 == 0 else 1
    step = group // chunks
    mixes = arrays[6].shape[1]
    wide = [v.transpose(1, 2, 0, 3).reshape(slab, rows, cells) for v in arrays[:4]]
    args = (*wide, arrays[4], arrays[5].T, arrays[6].transpose(1, 0, 2), *arrays[7:])
    vmem = pl.BlockSpec(memory_space=pltpu.VMEM)
    smem = pl.BlockSpec(memory_space=pltpu.SMEM)
    hbm = pl.BlockSpec(memory_space=pl.ANY)
    dma = pltpu.SemaphoreType.DMA
    out_t, out_d, border = pl.pallas_call(
        functools.partial(kernel, sizes, chunks, units),
        out_shape=(
            jax.ShapeDtypeStruct((slab, rows, cells), BF16),
            jax.ShapeDtypeStruct((slab, rows, cells), BF16),
            jax.ShapeDtypeStruct((1, cells), F32),
        ),
        in_specs=[hbm] * 4 + [vmem] * 2 + [hbm] * 2 + [smem],
        out_specs=(vmem, vmem, vmem),
        scratch_shapes=[
            *[pltpu.VMEM((slab, rows, cells), BF16)] * 4,
            pltpu.VMEM((mixes, rows, cells), BF16),
            pltpu.VMEM(arrays[7].shape, BF16),
            pltpu.VMEM((rows, full, cells), BF16),
            pltpu.VMEM((chunks, nz, step, full, cells), BF16),
            pltpu.VMEM((chunks, nz, step, full, cells), BF16),
            pltpu.VMEM((rows, full, cells), BF16),
            pltpu.VMEM((rows, cells), F32),
            pltpu.VMEM((nz * full, nz * full), BF16),
            pltpu.VMEM((full * (rows + 2 * MARGIN), cells), F32),
            pltpu.VMEM((full * rows, cells), F32),
            pltpu.VMEM((full, rows, cells), F32),
            pltpu.VMEM((2, full, cells), BF16),
            pltpu.VMEM((2, 2, rows, cells), BF16),
            pltpu.VMEM((2, 2, rows, cells), BF16),
            pltpu.VMEM((2, 2, rows, cells), F32),
            pltpu.VMEM((3, 8, cells), F32),
            pltpu.VMEM((nz, 8, cells), F32),
            pltpu.VMEM((ny, 8, cells), F32),
            pltpu.VMEM((nx, 8, cells), F32),
            dma((6,)),
            dma((chunks, nz)),
            dma((chunks, nz)),
            dma((chunks, nz)),
            dma((chunks, nz)),
            dma((2,)),
            dma((2,)),
            dma((2,)),
            dma((2,)),
            dma((nx + ny + nz - 3,)),
            dma((nz,)),
            dma((ny,)),
            dma((nx,)),
        ],
        compiler_params=pltpu.CompilerParams(
            collective_id=0, has_side_effects=True, vmem_limit_bytes=52 * 1024 * 1024
        ),
    )(*args)
    outs = [
        v.reshape(units, layers, rows, cells).transpose(2, 0, 1, 3) for v in (out_t, out_d)
    ]
    return (*outs, border[0, :3])


def solution(mesh):
    wide = P("tx", None, "lz", "ty")
    in_specs = (
        wide, wide, wide, wide, P("tx", "ty"), P("tx", "ty"), P("tx", None, "ty"), P(), P(),
    )
    sizes = tuple(mesh.shape[name] for name in ("tx", "ty", "lz"))
    return jax.shard_map(
        functools.partial(body, sizes), mesh=mesh, in_specs=in_specs,
        out_specs=(wide, wide, P()), check_vma=False,
    )
```

```python
import functools
import jax
import jax.numpy as jnp
from jax import lax
from jax.experimental import pallas as pl
from jax.experimental.pallas import tpu as pltpu
from jax.sharding import PartitionSpec as P

MESH = pl.DeviceIdType.MESH
F32 = jnp.float32
BF16 = jnp.bfloat16


MARGIN = 8


def kernel(
    sizes, chunks, units,
    test_hbm, dir_hbm, b_hbm, c_hbm, land_ref, active_ref, blocks_hbm, k_hbm, kappa_ref,
    out_t, out_d, border_ref,
    test_ref, dir_ref, b_ref, c_ref, blocks_ref, k_ref,
    masked, arrived, product, coupled, weight, big_k, field, back, before_image, halo,
    edge_out, edge_in, edge_f, stat_out, stat_z, stat_y,
    ls, fs, fr, bs, br, xs, xr, ys, yr, ss, sr_z, sr_y,
):
    nx, ny, nz = sizes
    slab, rows, cells = test_ref.shape
    layers = slab // units
    full = 2 * slab
    group = rows // nz
    step = group // chunks
    pitch = rows + 2 * MARGIN
    mx, my, mz = lax.axis_index("tx"), lax.axis_index("ty"), lax.axis_index("lz")
    fields = (test_ref, dir_ref)
    outs = (out_t, out_d)

    loads = [
        pltpu.make_async_copy(source, target, ls.at[i])
        for i, (source, target) in enumerate((
            (test_hbm, test_ref), (dir_hbm, dir_ref), (k_hbm, k_ref), (b_hbm, b_ref),
            (c_hbm, c_ref), (blocks_hbm, blocks_ref),
        ))
    ]
    for load in loads:
        load.start()

    barrier = pltpu.get_barrier_semaphore()
    for k in range(1, nz):
        pl.semaphore_signal(
            barrier, inc=1, device_id={"lz": lax.rem(mz + k, nz)}, device_id_type=MESH
        )
    for k in range(1, nx * ny):
        near = {"ty": lax.rem(my + k // nx, ny), "tx": lax.rem(mx + k % nx, nx)}
        pl.semaphore_signal(barrier, inc=1, device_id=near, device_id_type=MESH)

    lane = lax.broadcasted_iota(jnp.int32, (rows, cells), 1)
    line = lax.broadcasted_iota(jnp.int32, (rows, rows), 0)
    named = jnp.max(
        jnp.where(jnp.broadcast_to(active_ref[...], (rows, rows)) == line, 1.0, 0.0),
        axis=1, keepdims=True,
    )
    weight[...] = land_ref[...].astype(F32) * named
    ocean = weight[...]

    def middle(q):
        return pl.ds(pl.multiple_of(q * pitch + MARGIN, 8), rows)

    for f in range(2):
        loads[f].wait()

        def mask(j, carry):
            field[middle(f * slab + j), :] = fields[f][j].astype(F32) * ocean
            return carry

        lax.fori_loop(0, slab, mask, 0, unroll=8)

    def pack(c):
        def pack_row(i, carry):
            x = lax.div(i, step) * group + c * step + lax.rem(i, step)
            masked[x] = field[pl.ds(MARGIN + x, full, stride=pitch), :].astype(BF16)
            return carry

        lax.fori_loop(0, nz * step, pack_row, 0, unroll=4)

    pack(0)

    pl.semaphore_wait(barrier, nx * ny + nz - 2)

    def forward(c, k):
        to = lax.rem(mz + k, nz)
        return pltpu.make_async_remote_copy(
            src_ref=masked.at[pl.ds(to * group + c * step, step)],
            dst_ref=arrived.at[c, mz],
            send_sem=fs.at[c, to],
            recv_sem=fr.at[c, mz],
            device_id={"lz": to},
            device_id_type=MESH,
        )

    def forward_in(c, k):
        src = lax.rem(mz + nz - k, nz)
        return pltpu.make_async_remote_copy(
            src_ref=arrived.at[c, src],
            dst_ref=arrived.at[c, src],
            send_sem=fs.at[c, src],
            recv_sem=fr.at[c, src],
            device_id={"lz": src},
            device_id_type=MESH,
        )

    def backward(c, k):
        to = lax.rem(mz + k, nz)
        return pltpu.make_async_remote_copy(
            src_ref=product.at[c, to],
            dst_ref=coupled.at[pl.ds(mz * group + c * step, step)],
            send_sem=bs.at[c, to],
            recv_sem=br.at[c, mz],
            device_id={"lz": to},
            device_id_type=MESH,
        )

    def backward_in(c, k):
        src = lax.rem(mz + nz - k, nz)
        return pltpu.make_async_remote_copy(
            src_ref=product.at[c, src],
            dst_ref=coupled.at[pl.ds(src * group + c * step, step)],
            send_sem=bs.at[c, src],
            recv_sem=br.at[c, src],
            device_id={"lz": src},
            device_id_type=MESH,
        )

    order = sorted(range(1, nz), key=lambda k: -min(k, nz - k))
    for c in range(1, chunks):
        pack(c)
        for k in order:
            forward(c - 1, k).start()

    def own_row(i, carry):
        arrived[lax.div(i, step), mz, lax.rem(i, step)] = masked[mz * group + i]
        return carry

    lax.fori_loop(0, group, own_row, 0)
    for k in order:
        forward(chunks - 1, k).start()
    later, before = lax.rem(mx + 1, nx), lax.rem(mx + nx - 1, nx)
    to_later = pltpu.make_async_remote_copy(
        src_ref=masked.at[rows - 1], dst_ref=halo.at[0], send_sem=xs.at[0], recv_sem=xr.at[0],
        device_id={"tx": later}, device_id_type=MESH,
    )
    to_before = pltpu.make_async_remote_copy(
        src_ref=masked.at[0], dst_ref=halo.at[1], send_sem=xs.at[1], recv_sem=xr.at[1],
        device_id={"tx": before}, device_id_type=MESH,
    )
    to_later.start()
    to_before.start()
    for f in range(2):
        def edges(j, carry):
            first, last = carry
            value = field[middle(f * slab + j), :]
            first = jnp.where(lane == j, pltpu.roll(value, j, 1), first)
            last = jnp.where(lane == j, pltpu.roll(value, j + 1, 1), last)
            return first, last

        blank = jnp.zeros((rows, cells), F32)
        first, last = lax.fori_loop(0, slab, edges, (blank, blank), unroll=4)
        edge_out[0, f] = first.astype(BF16)
        edge_out[1, f] = last.astype(BF16)

    up, down = lax.rem(my + 1, ny), lax.rem(my + ny - 1, ny)
    to_up = pltpu.make_async_remote_copy(
        src_ref=edge_out.at[1], dst_ref=edge_in.at[0], send_sem=ys.at[0], recv_sem=yr.at[0],
        device_id={"ty": up}, device_id_type=MESH,
    )
    to_down = pltpu.make_async_remote_copy(
        src_ref=edge_out.at[0], dst_ref=edge_in.at[1], send_sem=ys.at[1], recv_sem=yr.at[1],
        device_id={"ty": down}, device_id_type=MESH,
    )
    col = units * layers * nz
    wide = nz * full

    def chooser(shape, dim, f):
        i = lax.broadcasted_iota(jnp.int32, shape, dim)
        j = lax.broadcasted_iota(jnp.int32, shape, 1 - dim)
        part, rest = i // full, lax.rem(i, full)
        field, entry = rest // slab, lax.rem(rest, slab)
        unit, layer = entry // layers, lax.rem(entry, layers)
        target = unit * (layers * nz) + part * layers + layer
        return jnp.where((target == j) & (field == f), 1.0, 0.0).astype(BF16)

    loads[2].wait()
    dense = k_ref[...]
    total = None
    for f in range(2):
        left = jnp.dot(
            chooser((wide, col), 0, f), dense, preferred_element_type=F32
        ).astype(BF16)
        both = jnp.dot(left, chooser((col, wide), 1, f), preferred_element_type=F32)
        total = both if total is None else total + both
    big_k[...] = total.astype(BF16)
    to_up.start()
    to_down.start()

    for load in loads[3:]:
        load.wait()
    zero = jnp.zeros((rows, cells), F32)
    sums = (zero, zero, zero)

    def norms(j, carry):
        bb, cc, cv = carry
        b = b_ref[j].astype(F32)
        c = c_ref[j].astype(F32)
        return bb + b * b, cc + c * c, cv + c * test_ref[j].astype(F32)

    quarter = slab // chunks
    for c in range(chunks):
        for k in order:
            forward_in(c, k).wait_recv()
        part = jnp.concatenate(
            [arrived[c, :, r].reshape(wide, cells) for r in range(step)], axis=1
        )
        result = jnp.dot(big_k[...], part, preferred_element_type=F32).astype(BF16)
        for d in range(nz):
            for r in range(step):
                product[c, d, r] = result[d * full:(d + 1) * full, r * cells:(r + 1) * cells]
        sums = lax.fori_loop(c * quarter, (c + 1) * quarter, norms, sums, unroll=2)
        for k in order:
            backward(c, k).start()
        for r in range(step):
            coupled[mz * group + c * step + r] = product[c, mz, r]

    to_later.wait_recv()
    to_before.wait_recv()
    to_up.wait_recv()
    to_down.wait_recv()
    field[pl.ds(MARGIN - 1, full, stride=pitch), :] = halo[0].astype(F32)
    field[pl.ds(MARGIN + rows, full, stride=pitch), :] = halo[1].astype(F32)

    @pl.when(my > 0)
    def _():
        edge_f[0] = edge_in[0].astype(F32)

    @pl.when(my == 0)
    def _():
        edge_f[0] = jnp.zeros((2, rows, cells), F32)

    @pl.when(my < ny - 1)
    def _():
        edge_f[1] = edge_in[1].astype(F32)

    @pl.when(my == ny - 1)
    def _():
        edge_f[1] = jnp.zeros((2, rows, cells), F32)

    for f in range(2):
        for u in range(units):
            def local(z, carry):
                j = u * layers + z
                q = f * slab + j
                here = field[middle(q), :]
                south = jnp.where(
                    lane == 0, pltpu.roll(edge_f[0, f], lax.rem(cells - j, cells), 1),
                    pltpu.roll(here, 1, 1),
                )
                north = jnp.where(
                    lane == cells - 1, pltpu.roll(edge_f[1, f], cells - 1 - j, 1),
                    pltpu.roll(here, cells - 1, 1),
                )
                near = field[pl.ds(q * pitch + MARGIN - 1, rows), :]
                near = near + field[pl.ds(q * pitch + MARGIN + 1, rows), :]
                value = kappa_ref[u] * (near + south + north - 4.0 * here)
                for w in range(units):
                    value = value + blocks_ref[units * u + w].astype(F32) * field[
                        middle(f * slab + w * layers + z), :
                    ]
                before_image[q] = value
                return carry

            lax.fori_loop(0, layers, local, 0, unroll=2)

    def insert(x, carry):
        back[pl.ds(x, full, stride=rows), :] = coupled[x].astype(F32)
        return carry

    for c in range(chunks):
        for k in order:
            backward_in(c, k).wait_recv()

        def chunk_row(i, carry):
            return insert(lax.div(i, step) * group + c * step + lax.rem(i, step), carry)

        lax.fori_loop(0, nz * step, chunk_row, 0, unroll=4)

    def image(j, carry):
        ba, be = carry
        b = b_ref[j].astype(F32)
        images = []
        for f in range(2):
            q = f * slab + j
            coup = back[pl.ds(pl.multiple_of(q * rows, 8), rows), :]
            images.append(ocean * (coup + before_image[q]))
            outs[f][j] = images[f].astype(BF16)
        return ba + b * images[0], be + b * images[1]

    pair = lax.fori_loop(0, slab, image, (zero, zero), unroll=6)

    lines = [jnp.sum(v, axis=0, keepdims=True) for v in (*sums, *pair)]
    value = jnp.concatenate(lines + [jnp.zeros((3, cells), F32)], axis=0)
    base = 0
    plane = [(i, k) for i in range(ny) for k in range(nx)]
    stages = (
        ([{"lz": lax.rem(mz + k, nz)} for k in range(nz)], nz, stat_z, sr_z, mz,
         [lax.rem(mz + nz - k, nz) for k in range(nz)]),
        ([{"ty": lax.rem(my + i, ny), "tx": lax.rem(mx + k, nx)} for i, k in plane],
         ny * nx, stat_y, sr_y, my * nx + mx,
         [lax.rem(my + ny - i, ny) * nx + lax.rem(mx + nx - k, nx) for i, k in plane]),
    )
    sends = []
    for s, (peers, size, box, sem, me, sources) in enumerate(stages):
        stat_out[s] = value
        box[me] = value
        for k in range(1, size):
            copy = pltpu.make_async_remote_copy(
                src_ref=stat_out.at[s], dst_ref=box.at[me], send_sem=ss.at[base + k - 1],
                recv_sem=sem.at[me], device_id=peers[k], device_id_type=MESH,
            )
            copy.start()
            sends.append(copy)
        base += size - 1
        for k in range(1, size):
            src = sources[k]
            pltpu.make_async_remote_copy(
                src_ref=stat_out.at[s], dst_ref=box.at[src], send_sem=ss.at[0],
                recv_sem=sem.at[src], device_id=peers[k], device_id_type=MESH,
            ).wait_recv()
        value = box[0]
        for i in range(1, size):
            value = value + box[i]
    final = jnp.broadcast_to(jnp.sum(value, axis=1, keepdims=True), (8, cells))
    bb, cc, cv, ba, be = (final[i:i + 1] for i in range(5))
    line = lax.broadcasted_iota(jnp.int32, (1, cells), 1)
    top = jnp.where(line == 0, ba, jnp.where(line == 1, be, cv))
    low = jnp.where(line == 2, cc, bb)
    border_ref[...] = top / jnp.sqrt(low)

    for c in range(chunks):
        for k in order:
            forward(c, k).wait_send()
            backward(c, k).wait_send()
    to_later.wait_send()
    to_before.wait_send()
    to_up.wait_send()
    to_down.wait_send()
    for copy in sends:
        copy.wait_send()


def body(sizes, *arrays):
    nx, ny, nz = sizes
    rows, units, layers, cells = arrays[0].shape
    slab = units * layers
    full = 2 * slab
    group = rows // nz
    chunks = 4 if group % 4 == 0 else 1
    step = group // chunks
    mixes = arrays[6].shape[1]
    wide = [v.transpose(1, 2, 0, 3).reshape(slab, rows, cells) for v in arrays[:4]]
    args = (*wide, arrays[4], arrays[5].T, arrays[6].transpose(1, 0, 2), *arrays[7:])
    args = (*[pltpu.with_memory_space_constraint(v, pltpu.HBM) for v in args[:8]], args[8])
    vmem = pl.BlockSpec(memory_space=pltpu.VMEM)
    smem = pl.BlockSpec(memory_space=pltpu.SMEM)
    hbm = pl.BlockSpec(memory_space=pl.ANY)
    dma = pltpu.SemaphoreType.DMA
    out_t, out_d, border = pl.pallas_call(
        functools.partial(kernel, sizes, chunks, units),
        out_shape=(
            jax.ShapeDtypeStruct((slab, rows, cells), BF16),
            jax.ShapeDtypeStruct((slab, rows, cells), BF16),
            jax.ShapeDtypeStruct((1, cells), F32),
        ),
        in_specs=[hbm] * 4 + [vmem] * 2 + [hbm] * 2 + [smem],
        out_specs=(vmem, vmem, vmem),
        scratch_shapes=[
            *[pltpu.VMEM((slab, rows, cells), BF16)] * 4,
            pltpu.VMEM((mixes, rows, cells), BF16),
            pltpu.VMEM(arrays[7].shape, BF16),
            pltpu.VMEM((rows, full, cells), BF16),
            pltpu.VMEM((chunks, nz, step, full, cells), BF16),
            pltpu.VMEM((chunks, nz, step, full, cells), BF16),
            pltpu.VMEM((rows, full, cells), BF16),
            pltpu.VMEM((rows, cells), F32),
            pltpu.VMEM((nz * full, nz * full), BF16),
            pltpu.VMEM((full * (rows + 2 * MARGIN), cells), F32),
            pltpu.VMEM((full * rows, cells), F32),
            pltpu.VMEM((full, rows, cells), F32),
            pltpu.VMEM((2, full, cells), BF16),
            pltpu.VMEM((2, 2, rows, cells), BF16),
            pltpu.VMEM((2, 2, rows, cells), BF16),
            pltpu.VMEM((2, 2, rows, cells), F32),
            pltpu.VMEM((2, 8, cells), F32),
            pltpu.VMEM((nz, 8, cells), F32),
            pltpu.VMEM((ny * nx, 8, cells), F32),
            dma((6,)),
            dma((chunks, nz)),
            dma((chunks, nz)),
            dma((chunks, nz)),
            dma((chunks, nz)),
            dma((2,)),
            dma((2,)),
            dma((2,)),
            dma((2,)),
            dma((nx * ny + nz - 2,)),
            dma((nz,)),
            dma((ny * nx,)),
        ],
        compiler_params=pltpu.CompilerParams(
            collective_id=0, has_side_effects=True, vmem_limit_bytes=52 * 1024 * 1024
        ),
    )(*args)
    outs = [
        v.reshape(units, layers, rows, cells).transpose(2, 0, 1, 3) for v in (out_t, out_d)
    ]
    return (*outs, border[0, :3])


def solution(mesh):
    wide = P("tx", None, "lz", "ty")
    in_specs = (
        wide, wide, wide, wide, P("tx", "ty"), P("tx", "ty"), P("tx", None, "ty"), P(), P(),
    )
    sizes = tuple(mesh.shape[name] for name in ("tx", "ty", "lz"))
    return jax.shard_map(
        functools.partial(body, sizes), mesh=mesh, in_specs=in_specs,
        out_specs=(wide, wide, P()), check_vma=False,
    )
```
